32 devices in a mesh: mem: 4 (over y, x), tile: 8 (over z, core).
Axes of the slice: x: 2, y: 2, z: 4, core: 2. Of those that a mesh axis runs over, the one named last changes fastest.
Arguments:
- ensemble: bfloat16 [32, 32, 128, 128], P('mem', None, 'tile'), may hold values from -0.75 to 0.75
- control: float32 [32, 16, 128, 128], P('mem', None, 'tile'), may hold values from -6 to 6
- level_loc: float32 [16, 16], replicated, may hold values from -0.35 to 1.25
- wind_speed: float32 [128, 128], P('tile'), may hold values from 0.1 to 0.35
- cell_codes: int32 [128, 128], P('tile'), may hold values from 0 to 2
- obs_cell: int32 [4096], P('tile'), may hold values from 0 to 2047
- innovation: float32 [32, 4096], P(None, 'tile'), may hold values from -12 to 12
- obs_sigma: float32 [32, 4096], P(None, 'tile'), may hold values from 0.5 to 2
Outputs:
- obs_gradient: float32 [32, 16, 128, 128], P('mem', None, 'tile')
The draws below stay inside these ranges and needn't reach their ends.
Inputs may be any that keep to these rules, and one draw needn't show every extreme that they name: obs_cell[j] counts cells within tile j // 512, as (x - tile's first x) * 128 + y; several observations may share a cell. `cell_codes`: 0 is an open cell, 1 a wall cell that no flux enters or leaves, 2 an open cell that keeps 0.7 of its value each step.
All inputs are finite; a program needn't handle non-finite values.
Results may differ from the reference program's by a relative error of at most 0.0003.
Values may be sent and summed in bfloat16 or wider, within the bound.
A program may use at most 64 MiB of HBM per device.

```python
import math
import jax
import jax.numpy as jnp
from jax import lax

K_DEV = 8
L = 16
V = 2
CX = 16
NY = 128
STEPS = 2
VL = 32
MEMBERS = 32
NX = 128
NOBS = 512
TOTAL_OBS = 4096
N_MEM = 4
N_TILE = 8


def draw_ensemble(key, part):
    shape = (MEMBERS, V * L, NX, NY)
    values = 0.125 * jax.random.truncated_normal(key, -6.0, 6.0, shape, jnp.float32)
    return values.astype(jnp.bfloat16)


def draw_control(key, part):
    shape = (MEMBERS, L, NX, NY)
    values = jax.random.truncated_normal(key, -6.0, 6.0, shape, jnp.float32)
    return values


def draw_level_loc(key, part):
    first_key, second_key = jax.random.split(key)
    rows = jnp.arange(L, dtype=jnp.int32)[:, None]
    cols = jnp.arange(L, dtype=jnp.int32)[None, :]
    dist = jnp.abs(rows - cols).astype(jnp.float32)
    off = jax.random.uniform(first_key, (L, L), jnp.float32, -1.0, 1.0)
    diag = jax.random.uniform(second_key, (L, L), jnp.float32, 0.8, 1.2)
    off_part = 0.35 * off * jnp.exp(-dist / 3.0)
    return jnp.where(dist == 0.0, diag, off_part).astype(jnp.float32)


def plant(values, own_key, least, largest):
    longest = values.shape.index(max(values.shape))
    spots = []
    for shift in (0, 1):
        where = [jax.random.randint(jax.random.fold_in(own_key, axis), (), 0, length) for axis, length in enumerate(values.shape)]
        where[longest] = (where[longest] + shift) % values.shape[longest]
        spots.append(tuple(where))
    return values.at[spots[0]].set(least).at[spots[1]].set(largest)


def levels(rng, dims, cuts, smallest, high):
    def one(position, blocks):
        draws = jax.random.uniform(jax.random.fold_in(jax.random.fold_in(rng, 6), position), (blocks,), jnp.float32, smallest / len(cuts), high / len(cuts))
        return jnp.repeat(jnp.exp(draws), dims[position] // blocks).reshape((-1,) + (1,) * (len(dims) - position - 1))

    level = one(*cuts[0])
    for cut in cuts[1:]:
        level = level * one(*cut)
    return level


def noise(key, dims, spread, reach, cuts=(), kind=jnp.bfloat16):
    result = jax.random.normal(key, dims, jnp.float32) * spread
    if len(cuts) > 0:
        result = levels(key, dims, cuts, -0.22, 0.18) * result
    return jnp.clip(result, min=-reach, max=reach).astype(kind)


def setup_inputs(seed: int = 0) -> dict:
    key_of = jax.random.split(jax.random.key(seed), 9)
    ensemble = draw_ensemble(jax.random.fold_in(key_of[8], 71), 0)
    control = draw_control(jax.random.fold_in(key_of[8], 71), 0)
    level_loc = draw_level_loc(jax.random.fold_in(key_of[8], 71), 0)
    wind_speed = jnp.clip(0.1 + 0.25 * jax.random.uniform(key_of[3], (NX, NY), jnp.float32) ** levels(key_of[3], (NX, NY), ((0, 8),), -0.2, 0.2), 0.1, 0.35)
    cell_codes = plant(jax.random.randint(key_of[4], (NX, NY), 0, 3), jax.random.fold_in(key_of[4], 1), 0, 2).astype(jnp.int32)
    obs_cell = plant(jax.random.randint(key_of[5], (TOTAL_OBS,), 0, CX * NY), jax.random.fold_in(key_of[5], 1), 0, (CX * NY) - 1).astype(jnp.int32)
    innovation = noise(key_of[6], (VL, TOTAL_OBS), 2.0, 12.0, ((1, 8),), jnp.float32)
    obs_sigma = jnp.clip(jnp.exp(math.log(2.0) - 1.3862944 * jax.random.uniform(key_of[7], (VL, TOTAL_OBS), jnp.float32) ** levels(key_of[7], (VL, TOTAL_OBS), ((1, 8),), -0.2, 0.2)), 0.5, 2.0)
    return {"ensemble": ensemble, "control": control, "level_loc": level_loc, "wind_speed": wind_speed, "cell_codes": cell_codes, "obs_cell": obs_cell, "innovation": innovation, "obs_sigma": obs_sigma}


diffusion_rate = 0.12
absorbing = 0.7
step_length = 0.5
huber_delta = 1.0


def smooth_field(values):
    padded = jnp.pad(values, [(0, 0)] * (values.ndim - 2) + [(1, 1), (1, 1)])
    along_x = 0.5 * padded[..., 1:-1, :] + 0.25 * (padded[..., :-2, :] + padded[..., 2:, :])
    return 0.5 * along_x[..., 1:-1] + 0.25 * (along_x[..., :-2] + along_x[..., 2:])


def make_coeffs(open_cells, wind_speed):
    rate = diffusion_rate
    open_east = open_cells * jnp.pad(open_cells[1:], ((0, 1), (0, 0)))
    open_west = jnp.pad(open_east[:-1], ((1, 0), (0, 0)))
    open_north = open_cells * jnp.pad(open_cells[:, 1:], ((0, 0), (0, 1)))
    open_south = jnp.pad(open_north[:, :-1], ((0, 0), (1, 0)))
    wind_west = jnp.pad(wind_speed[:-1], ((1, 0), (0, 0)))
    center = 1.0 - rate * (open_east + open_west + open_north + open_south) - wind_speed * open_east
    forward = (center, (rate + wind_west) * open_west, rate * open_east, rate * open_south, rate * open_north)
    adjoint = (center, rate * open_west, (rate + wind_speed) * open_east, rate * open_south, rate * open_north)
    return forward, adjoint


def apply_stencil(state_field, coeffs):
    center, west_coef, east_coef, south_coef, north_coef = coeffs
    padded = jnp.pad(state_field, ((0, 0), (1, 1), (1, 1)))
    return (center * state_field + west_coef * padded[:, :-2, 1:-1] + east_coef * padded[:, 2:, 1:-1]
            + south_coef * padded[:, 1:-1, :-2] + north_coef * padded[:, 1:-1, 2:])


def reference(ensemble, control, level_loc, wind_speed, cell_codes, obs_cell, innovation, obs_sigma):
    highest = lax.Precision.HIGHEST
    open_cells = (cell_codes != 1).astype(jnp.float32)
    absorb = jnp.where(cell_codes == 2, absorbing, 1.0).astype(jnp.float32)
    forward, adjoint = make_coeffs(open_cells, wind_speed)
    tile_of = jnp.arange(NOBS * N_TILE, dtype=jnp.int32) // NOBS
    flat_index = (tile_of * (CX * NY) + obs_cell).astype(jnp.int32)
    ens_blocks = ensemble.reshape(N_MEM, K_DEV, V, L, NX, NY)

    def localize(block_weights):
        level_mixed = jnp.einsum("ml,klxy->kmxy", level_loc, block_weights, precision=highest)
        return smooth_field(level_mixed)

    def evaluate(weight_blocks):
        def accumulate(total, pair):
            ens_block, block_weights = pair
            mixed = localize(block_weights)
            return total + jnp.sum(ens_block.astype(jnp.float32) * mixed[:, None], 0), None

        increment, _ = lax.scan(accumulate, jnp.zeros((V, L, NX, NY), jnp.float32), (ens_blocks, weight_blocks))
        state_field = increment.reshape(VL, NX, NY)
        for sweep_index in range(STEPS):
            state_field = absorb * apply_stencil(state_field, forward)
        sampled = state_field.reshape(VL, NX * NY)[:, flat_index]
        scaled = (sampled - innovation) / obs_sigma
        obs_weight = jnp.clip(scaled, -huber_delta, huber_delta) / obs_sigma
        gridded = jnp.zeros((VL, NX * NY), jnp.float32).at[:, flat_index].add(obs_weight)
        adjoint_field = gridded.reshape(VL, NX, NY)
        for sweep_index in range(STEPS):
            adjoint_field = apply_stencil(absorb * adjoint_field, adjoint)
        adjoint_field = adjoint_field.reshape(V, L, NX, NY)

        def project(ens_block):
            member_term = jnp.sum(ens_block.astype(jnp.float32) * adjoint_field[None], 1)
            level_mix = jnp.einsum("ml,kmxy->klxy", level_loc, member_term, precision=highest)
            return smooth_field(level_mix)

        return lax.map(project, ens_blocks)

    control_blocks = control.reshape(N_MEM, K_DEV, L, NX, NY)
    first = evaluate(control_blocks)
    next_control = control_blocks - step_length * (control_blocks + first)
    second = evaluate(next_control)
    return second.reshape(MEMBERS, L, NX, NY)
```

```python
import functools

import jax
import jax.numpy as jnp
from jax import lax
from jax.experimental import pallas as pl
from jax.experimental.pallas import tpu as pltpu
from jax.sharding import PartitionSpec as P

V = 2
STEPS = 2
HALO = 8

diffusion_rate = 0.12
absorbing = 0.7
step_length = 0.5
huber_delta = 1.0

MESH = pl.DeviceIdType.MESH
F32 = jnp.float32
BF16 = jnp.bfloat16
HIGHEST = lax.Precision.HIGHEST
NT = (((1,), (1,)), ((), ()))


def log2(n):
    assert n & (n - 1) == 0
    return n.bit_length() - 1


def iota(shape, dim):
    return lax.broadcasted_iota(jnp.int32, shape, dim)


def split(x):
    hi = x.astype(BF16)
    return hi, (x - hi.astype(F32)).astype(BF16)


def mm(a, b):
    return jnp.dot(a, b, preferred_element_type=F32)


def dot3(a, b):
    ah, al = a
    bh, bl = split(b)
    return mm(ah, bh) + (mm(ah, bl) + mm(al, bh))


def kernel(
    n_mem, n_tile, members, levels, width, ny, nobs,
    ens, ctl, loc, wind, codes, cell, innov, sigma,
    out,
    ensf, work, nxt, mats, small,
    ctl_stage, ctl_halo, codes_halo, wind_halo, cell_halo, innov_halo, sigma_halo,
    ens_stage, ens_halo,
    part, rs_buf, inc, inc_halo, ext, adj_stage, ag, edge_stage, agh,
    r0_send, r0_recv, rs_send, rs_recv, h_send, h_recv, ag_send, ag_recv, e_send, e_recv,
):
    m = lax.axis_index("mem")
    t = lax.axis_index("tile")
    has = (t > 0, t < n_tile - 1)
    rows = V * levels
    share = rows // n_mem
    block = levels * width
    xs = log2(width)

    def tell(dev):
        pl.semaphore_signal(pltpu.get_barrier_semaphore(), inc=1, device_id=dev, device_id_type=MESH)

    for d in range(1, n_mem):
        tell((lax.rem(m + d, n_mem), t))

    @pl.when(has[0])
    def _():
        tell((m, t - 1))

    @pl.when(has[1])
    def _():
        tell((m, t + 1))

    kl = members * levels
    ctl_stage[0] = ctl[pl.ds(width - 1, kl, stride=width), :]
    ctl_stage[1] = ctl[pl.ds(0, kl, stride=width), :]

    peers = n_mem - 1 + jnp.where(t > 0, 1, 0) + jnp.where(t < n_tile - 1, 1, 0)
    pl.semaphore_wait(pltpu.get_barrier_semaphore(), peers)

    def to_side(side, src, dst, ssem, rsem):
        dev = (m, t + 1) if side == 0 else (m, t - 1)
        return pltpu.make_async_remote_copy(
            src_ref=src, dst_ref=dst, send_sem=ssem, recv_sem=rsem, device_id=dev, device_id_type=MESH
        )

    mine = pl.ds(m * share, share)
    near = (pl.ds(width - HALO, HALO), pl.ds(0, HALO))
    first_msgs = []
    for side in (0, 1):
        pairs = [
            (ctl_stage.at[side], ctl_halo.at[side]),
            (codes.at[near[side]], codes_halo.at[side]),
            (wind.at[near[side]], wind_halo.at[side]),
            (cell, cell_halo.at[side]),
            (innov.at[m], innov_halo.at[side]),
            (sigma.at[m], sigma_halo.at[side]),
            (ens_stage.at[side], ens_halo.at[side]),
        ]
        first_msgs.append(
            [to_side(side, s, d, r0_send.at[side, i], r0_recv.at[side, i]) for i, (s, d) in enumerate(pairs)]
        )

    def start_side(side, which):
        @pl.when(has[1 - side])
        def _():
            for i in which:
                first_msgs[side][i].start()

    def recv_side(side, which):
        @pl.when(has[side])
        def _():
            for i in which:
                first_msgs[side][i].wait_recv()

    for side in (0, 1):
        start_side(side, (0,))
    for side in (0, 1):
        start_side(side, (1, 2, 3, 4, 5))

        @pl.when(jnp.logical_not(has[side]))
        def _():
            ctl_halo[side] = jnp.zeros_like(ctl_halo[side])
            codes_halo[side] = jnp.ones_like(codes_halo[side])
            wind_halo[side] = jnp.zeros_like(wind_halo[side])
            cell_halo[side] = jnp.full_like(cell_halo[side], -1)
            innov_halo[side] = jnp.zeros_like(innov_halo[side])
            sigma_halo[side] = jnp.ones_like(sigma_halo[side])
            ens_halo[side] = jnp.zeros_like(ens_halo[side])
            for e in (0, 1):
                inc_halo[e, side] = jnp.zeros_like(inc_halo[e, side])

    lo = loc[...]
    pick = (iota((block, levels), 0) >> xs == iota((block, levels), 1)).astype(F32)
    xr, xc = iota((block, block), 0) & (width - 1), iota((block, block), 1) & (width - 1)
    near_x = jnp.where(xr == xc, 0.5, jnp.where(jnp.abs(xr - xc) == 1, 0.25, 0.0)).astype(F32)
    ls = log2(levels)
    pick2 = ((iota((kl, levels), 0) & (levels - 1)) == iota((kl, levels), 1)).astype(F32)
    same_k = ((iota((kl, kl), 0) >> ls) == (iota((kl, kl), 1) >> ls)).astype(F32)

    def nt(a, b):
        return lax.dot_general(a, b, NT, precision=HIGHEST, preferred_element_type=F32)

    for i in (0, 1):
        def left(p):
            return jnp.dot(p, lo, precision=HIGHEST, preferred_element_type=F32) if i == 0 else nt(p, lo)

        hi, low = split(nt(left(pick), pick) * near_x)
        mats[i, 0] = hi
        mats[i, 1] = low
        hi, low = split(nt(left(pick2), pick2) * same_k)
        small[i, 0] = hi
        small[i, 1] = low

    yi = iota((1, ny), 1)
    from_south = jnp.where(yi > 0, 0.25, 0.0).astype(F32)
    from_north = jnp.where(yi < ny - 1, 0.25, 0.0).astype(F32)

    def smooth_y(v):
        return 0.5 * v + (from_south * pltpu.roll(v, 1, 1) + from_north * pltpu.roll(v, ny - 1, 1))

    def mix(src, i, edges):
        big = (mats[i, 0], mats[i, 1])
        for k in range(0, members, 2):
            both = jnp.concatenate(
                [src[k * block:(k + 1) * block, :], src[(k + 1) * block:(k + 2) * block, :]], axis=1
            )
            done = dot3(big, both)
            work[k * block:(k + 1) * block, :] = done[:, :ny]
            work[(k + 1) * block:(k + 2) * block, :] = done[:, ny:]
        side = dot3((small[i, 0], small[i, 1]), jnp.concatenate(edges(), axis=1))
        for j, x in ((0, 0), (1, width - 1)):
            at = pl.ds(x, kl, stride=width)
            work[at, :] = work[at, :] + 0.25 * side[:, j * ny:(j + 1) * ny]
        return side

    def send_mem(d, src, dst, ssem, rsem):
        return pltpu.make_async_remote_copy(
            src_ref=src, dst_ref=dst, send_sem=ssem, recv_sem=rsem,
            device_id=(lax.rem(m + d, n_mem), t), device_id_type=MESH,
        )

    def coefficients():
        code = jnp.concatenate([codes_halo[0], codes[...], codes_halo[1]], axis=0)
        speed = jnp.concatenate([wind_halo[0], wind[...], wind_halo[1]], axis=0)
        n = code.shape[0]
        opened = (code != 1).astype(F32)
        absorb = jnp.where(code == 2, absorbing, 1.0).astype(F32)
        yy = iota(code.shape, 1)
        oe = opened * pltpu.roll(opened, n - 1, 0)
        ow = opened * pltpu.roll(opened, 1, 0)
        on = jnp.where(yy < ny - 1, opened * pltpu.roll(opened, ny - 1, 1), 0.0)
        os = jnp.where(yy > 0, opened * pltpu.roll(opened, 1, 1), 0.0)
        k = diffusion_rate
        center = 1.0 - k * (oe + ow + on + os) - speed * oe
        fwd = (center, (k + pltpu.roll(speed, 1, 0)) * ow, k * oe, k * os, k * on)
        adj = (center, k * ow, (k + speed) * oe, k * os, k * on)
        return absorb, fwd, adj

    def stencil(q, coef):
        center, west, east, south, north = coef
        n = q.shape[0]
        return (
            center * q
            + west * pltpu.roll(q, 1, 0)
            + east * pltpu.roll(q, n - 1, 0)
            + south * pltpu.roll(q, 1, 1)
            + north * pltpu.roll(q, ny - 1, 1)
        )

    def observe(field, e):
        state = jnp.stack(field, axis=0)
        tiles = (
            (cell_halo[0], innov_halo[0], sigma_halo[0], 0, HALO, width - HALO),
            (cell[...], innov[m], sigma[m], HALO, width, 0),
            (cell_halo[1], innov_halo[1], sigma_halo[1], HALO + width, HALO, 0),
        )
        pieces = []
        for where, seen, dev, at, count, offset in tiles:
            hot_y = (iota((ny, nobs), 0) == (where & (ny - 1))).astype(BF16)
            hot_x = (iota((count, nobs), 0) == ((where >> log2(ny)) - offset)).astype(F32)
            part_state = state[:, at:at + count, :].reshape(share * count, ny)
            hi, low = split(part_state)
            got = (mm(hi, hot_y) + mm(low, hot_y)).reshape(share, count, nobs)
            sampled = jnp.sum(got * hot_x[None], axis=1)
            scaled = (sampled - seen) / dev
            weight = jnp.clip(scaled, -huber_delta, huber_delta) / dev
            hi, low = split(weight)
            total = None
            for w in (hi, low):
                spread = (w.astype(F32)[:, None, :] * hot_x[None]).reshape(share * count, nobs).astype(BF16)
                put = lax.dot_general(spread, hot_y, NT, preferred_element_type=F32)
                total = put if total is None else total + put
            pieces.append(total.reshape(share, count, ny))
        return jnp.concatenate(pieces, axis=1)


    def evaluate(e, src, edges):
        mix(src, 0, edges)
        for k in range(members):
            at = pl.ds(k * block, block)
            work[at, :] = smooth_y(work[at, :])
        copies = []
        for d in list(range(1, n_mem)) + [0]:
            who = lax.rem(m + d, n_mem)
            r0 = who * share
            l0 = lax.rem(r0, levels)
            total = jnp.zeros((share, width, ny), F32)
            for k in range(members):
                a = work[pl.ds(pl.multiple_of(k * block + l0 * width, width), share * width), :]
                total += ens[k, pl.ds(r0, share)].astype(F32) * a.reshape(share, width, ny)
            part[e, d] = total
            if d:
                copy = send_mem(d, part.at[e, d], rs_buf.at[e, d], rs_send.at[e, d], rs_recv.at[e, d])
                copy.start()
                copies.append(copy)
        if e == 0:
            for k in range(members):
                ensf[pl.ds(k * rows * width, rows * width), :] = (
                    ens[k].astype(F32).reshape(rows * width, ny)
                )
            for i in (0, 1):
                ens_stage[0, i] = ensf[pl.ds(width - 2 + i, members * rows, stride=width), :].astype(BF16)
                ens_stage[1, i] = ensf[pl.ds(i, members * rows, stride=width), :].astype(BF16)
            for side in (0, 1):
                start_side(side, (6,))
            for side in (0, 1):
                recv_side(side, (1, 2, 3, 4, 5))
        for copy in copies:
            copy.wait_recv()
        total = part[e, 0]
        for d in range(1, n_mem):
            total = total + rs_buf[e, d]
        inc[e, 0] = total[:, width - HALO:, :]
        inc[e, 1] = total[:, :HALO, :]
        halo = [
            to_side(side, inc.at[e, side], inc_halo.at[e, side], h_send.at[e, side], h_recv.at[e, side])
            for side in (0, 1)
        ]
        for side in (0, 1):
            @pl.when(has[1 - side])
            def _():
                halo[side].start()
        absorb, fwd, adj = coefficients()
        for side in (0, 1):
            @pl.when(has[side])
            def _():
                halo[side].wait_recv()
        whole = jnp.concatenate([inc_halo[e, 0], total, inc_halo[e, 1]], axis=1)
        n = HALO + width + HALO
        fields = [whole[r] for r in range(share)]
        for _ in range(STEPS):
            fields = [absorb * stencil(q, fwd) for q in fields]
        gridded = observe(fields, e)
        fields = [gridded[r] for r in range(share)]
        for _ in range(STEPS):
            fields = [stencil(absorb * p, adj) for p in fields]
        for r in range(share):
            ext[pl.ds(r * n, n), :] = fields[r]
            adj_stage[e, r] = fields[r][HALO:HALO + width]
            ag[e, m, r] = fields[r][HALO:HALO + width]
        for i, row in enumerate((HALO - 2, HALO - 1, HALO + width, HALO + width + 1)):
            v = ext[pl.ds(row, share, stride=n), :]
            edge_stage[e, i] = v
            agh[e, m, i] = v
        gathers = []
        for d in range(1, n_mem):
            gathers.append(send_mem(d, adj_stage.at[e], ag.at[e, m], ag_send.at[e, d], ag_recv.at[e, d]))
            gathers.append(send_mem(d, edge_stage.at[e], agh.at[e, m], e_send.at[e, d], e_recv.at[e, d]))
        for copy in gathers:
            copy.start()
        if e == 0:
            for side in (0, 1):
                recv_side(side, (6,))
        for copy in gathers:
            copy.wait_recv()
        half = levels * width
        whole = ag[e].reshape(rows * width, ny)
        for k in range(members):
            at = k * rows * width
            nxt[pl.ds(k * block, block), :] = (
                ensf[pl.ds(at, half), :] * whole[:half] + ensf[pl.ds(at + half, half), :] * whole[half:]
            )
        terms = []
        for i in range(4):
            a = agh[e, :, i].reshape(1, rows, ny)
            p = ens_halo[i // 2, i % 2].astype(F32).reshape(members, rows, ny) * a
            terms.append((p[:, :levels] + p[:, levels:]).reshape(kl, ny))

        def term_edges():
            parts = [terms[1], terms[2]]
            if e == 0:
                row0 = nxt[pl.ds(0, kl, stride=width), :]
                row1 = nxt[pl.ds(width - 1, kl, stride=width), :]
                parts.append(0.5 * terms[1] + 0.25 * (terms[0] + row0))
                parts.append(0.5 * terms[2] + 0.25 * (terms[3] + row1))
            return parts

        side = mix(nxt, 1, term_edges)

        def drain():
            for copy in copies + gathers:
                copy.wait_send()
            for s in (0, 1):
                @pl.when(has[1 - s])
                def _():
                    halo[s].wait_send()

        return side, drain

    def control_edges():
        for side in (0, 1):
            recv_side(side, (0,))
        return [ctl_halo[0], ctl_halo[1]]

    side, drain0 = evaluate(0, ctl, control_edges)
    outer = []
    for s in (0, 1):
        f = smooth_y(side[:, (2 + s) * ny:(3 + s) * ny])
        c = ctl_halo[s]
        inside = jnp.where(has[s], 1.0, 0.0).astype(F32)
        outer.append((c - step_length * (c + f)) * inside)
    for k in range(members):
        at = pl.ds(k * block, block)
        c = ctl[at, :]
        nxt[at, :] = c - step_length * (c + smooth_y(work[at, :]))
    _, drain1 = evaluate(1, nxt, lambda: outer)
    for k in range(members):
        at = pl.ds(k * block, block)
        out[at, :] = smooth_y(work[at, :])
    drain0()
    drain1()
    for s in (0, 1):
        @pl.when(has[1 - s])
        def _():
            for copy in first_msgs[s]:
                copy.wait_send()


def body(n_mem, n_tile, ensemble, control, level_loc, wind_speed, cell_codes, obs_cell, innovation, obs_sigma):
    members, rows, width, ny = ensemble.shape
    levels = control.shape[1]
    nobs = obs_cell.shape[0]
    share = rows // n_mem
    kl = members * levels
    block = levels * width
    n = width + 2 * HALO
    vmem = pltpu.VMEM
    dma = pltpu.SemaphoreType.DMA
    scratch = [
        vmem((members * rows * width, ny), F32),
        vmem((members * block, ny), F32),
        vmem((members * block, ny), F32),
        vmem((2, 2, block, block), BF16),
        vmem((2, 2, kl, kl), BF16),
        vmem((2, kl, ny), F32),
        vmem((2, kl, ny), F32),
        vmem((2, HALO, ny), jnp.int32),
        vmem((2, HALO, ny), F32),
        vmem((2, 1, nobs), jnp.int32),
        vmem((2, share, nobs), F32),
        vmem((2, share, nobs), F32),
        vmem((2, 2, members * rows, ny), BF16),
        vmem((2, 2, members * rows, ny), BF16),
        vmem((2, n_mem, share, width, ny), F32),
        vmem((2, n_mem, share, width, ny), F32),
        vmem((2, 2, share, HALO, ny), F32),
        vmem((2, 2, share, HALO, ny), F32),
        vmem((share * n, ny), F32),
        vmem((2, share, width, ny), F32),
        vmem((2, n_mem, share, width, ny), F32),
        vmem((2, 4, share, ny), F32),
        vmem((2, n_mem, 4, share, ny), F32),
        dma((2, 7)), dma((2, 7)),
        dma((2, n_mem)), dma((2, n_mem)),
        dma((2, 2)), dma((2, 2)),
        dma((2, n_mem)), dma((2, n_mem)),
        dma((2, n_mem)), dma((2, n_mem)),
    ]
    whole = pl.BlockSpec(memory_space=pltpu.VMEM)
    result = pl.pallas_call(
        functools.partial(kernel, n_mem, n_tile, members, levels, width, ny, nobs),
        out_shape=jax.ShapeDtypeStruct((members * block, ny), F32),
        in_specs=[whole] * 8,
        out_specs=whole,
        scratch_shapes=scratch,
        compiler_params=pltpu.CompilerParams(
            collective_id=0, has_side_effects=True, vmem_limit_bytes=48 << 20
        ),
    )(
        ensemble,
        control.reshape(members * block, ny),
        level_loc,
        wind_speed,
        cell_codes,
        obs_cell.reshape(1, nobs),
        innovation.reshape(n_mem, share, nobs),
        obs_sigma.reshape(n_mem, share, nobs),
    )
    return result.reshape(members, levels, width, ny)


def solution(mesh):
    placed = (
        P("mem", None, "tile", None),
        P("mem", None, "tile", None),
        P(),
        P("tile", None),
        P("tile", None),
        P("tile"),
        P(None, "tile"),
        P(None, "tile"),
    )
    return jax.shard_map(
        functools.partial(body, mesh.shape["mem"], mesh.shape["tile"]),
        mesh=mesh, in_specs=placed, out_specs=P("mem", None, "tile", None), check_vma=False,
    )
```

```python
import functools

import jax
import jax.numpy as jnp
from jax import lax
from jax.experimental import pallas as pl
from jax.experimental.pallas import tpu as pltpu
from jax.sharding import PartitionSpec as P

V = 2
STEPS = 2
HALO = 8

diffusion_rate = 0.12
absorbing = 0.7
step_length = 0.5
huber_delta = 1.0

MESH = pl.DeviceIdType.MESH
F32 = jnp.float32
BF16 = jnp.bfloat16
HIGHEST = lax.Precision.HIGHEST
NT = (((1,), (1,)), ((), ()))


def log2(n):
    assert n & (n - 1) == 0
    return n.bit_length() - 1


def iota(shape, dim):
    return lax.broadcasted_iota(jnp.int32, shape, dim)


def split(x):
    hi = x.astype(BF16)
    return hi, (x - hi.astype(F32)).astype(BF16)


def mm(a, b):
    return jnp.dot(a, b, preferred_element_type=F32)


def dot3(a, b):
    ah, al = a
    bh, bl = split(b)
    return mm(ah, bh) + (mm(ah, bl) + mm(al, bh))


def kernel(
    n_mem, n_tile, members, levels, width, ny, nobs,
    ens_hbm, ctl_hbm, loc_hbm, wind_hbm, codes_hbm, cell_hbm, innov_hbm, sigma_hbm,
    out,
    ens, ctl, loc, wind, codes, cell, innov, sigma, in_sem,
    ensf, work, nxt, mats, small,
    ctl_stage, ctl_halo, codes_halo, wind_halo, cell_halo, innov_halo, sigma_halo,
    ens_stage, ens_halo,
    part, rs_buf, inc, inc_halo, ext, adj_stage, ag, edge_stage, agh,
    r0_send, r0_recv, rs_send, rs_recv, h_send, h_recv, ag_send, ag_recv, e_send, e_recv,
):
    m = lax.axis_index("mem")
    t = lax.axis_index("tile")
    has = (t > 0, t < n_tile - 1)
    rows = V * levels
    share = rows // n_mem
    block = levels * width
    xs = log2(width)

    def tell(dev):
        pl.semaphore_signal(pltpu.get_barrier_semaphore(), inc=1, device_id=dev, device_id_type=MESH)

    for d in range(1, n_mem):
        tell((lax.rem(m + d, n_mem), t))

    @pl.when(has[0])
    def _():
        tell((m, t - 1))

    @pl.when(has[1])
    def _():
        tell((m, t + 1))

    loads = [
        pltpu.make_async_copy(src, dst, in_sem.at[i])
        for i, (src, dst) in enumerate((
            (ctl_hbm, ctl), (loc_hbm, loc), (ens_hbm, ens), (wind_hbm, wind), (codes_hbm, codes),
            (cell_hbm, cell), (innov_hbm.at[m], innov), (sigma_hbm.at[m], sigma),
        ))
    ]
    for load in loads:
        load.start()
    loads[0].wait()

    kl = members * levels
    ctl_stage[0] = ctl[pl.ds(width - 1, kl, stride=width), :]
    ctl_stage[1] = ctl[pl.ds(0, kl, stride=width), :]

    peers = n_mem - 1 + jnp.where(t > 0, 1, 0) + jnp.where(t < n_tile - 1, 1, 0)
    pl.semaphore_wait(pltpu.get_barrier_semaphore(), peers)

    def to_side(side, src, dst, ssem, rsem):
        dev = (m, t + 1) if side == 0 else (m, t - 1)
        return pltpu.make_async_remote_copy(
            src_ref=src, dst_ref=dst, send_sem=ssem, recv_sem=rsem, device_id=dev, device_id_type=MESH
        )

    mine = pl.ds(m * share, share)
    near = (pl.ds(width - HALO, HALO), pl.ds(0, HALO))
    first_msgs = []
    for side in (0, 1):
        pairs = [
            (ctl_stage.at[side], ctl_halo.at[side]),
            (codes_hbm.at[near[side]], codes_halo.at[side]),
            (wind_hbm.at[near[side]], wind_halo.at[side]),
            (cell_hbm, cell_halo.at[side]),
            (innov_hbm.at[m], innov_halo.at[side]),
            (sigma_hbm.at[m], sigma_halo.at[side]),
            (ens_stage.at[side], ens_halo.at[side]),
        ]
        first_msgs.append(
            [to_side(side, s, d, r0_send.at[side, i], r0_recv.at[side, i]) for i, (s, d) in enumerate(pairs)]
        )

    def start_side(side, which):
        @pl.when(has[1 - side])
        def _():
            for i in which:
                first_msgs[side][i].start()

    def recv_side(side, which):
        @pl.when(has[side])
        def _():
            for i in which:
                first_msgs[side][i].wait_recv()

    for side in (0, 1):
        start_side(side, (0,))
    for side in (0, 1):
        start_side(side, (1, 2, 3, 4, 5))

        @pl.when(jnp.logical_not(has[side]))
        def _():
            ctl_halo[side] = jnp.zeros_like(ctl_halo[side])
            codes_halo[side] = jnp.ones_like(codes_halo[side])
            wind_halo[side] = jnp.zeros_like(wind_halo[side])
            cell_halo[side] = jnp.full_like(cell_halo[side], -1)
            innov_halo[side] = jnp.zeros_like(innov_halo[side])
            sigma_halo[side] = jnp.ones_like(sigma_halo[side])
            ens_halo[side] = jnp.zeros_like(ens_halo[side])
            for e in (0, 1):
                inc_halo[e, side] = jnp.zeros_like(inc_halo[e, side])

    loads[1].wait()
    lo = loc[...]
    pick = (iota((block, levels), 0) >> xs == iota((block, levels), 1)).astype(F32)
    xr, xc = iota((block, block), 0) & (width - 1), iota((block, block), 1) & (width - 1)
    near_x = jnp.where(xr == xc, 0.5, jnp.where(jnp.abs(xr - xc) == 1, 0.25, 0.0)).astype(F32)
    ls = log2(levels)
    pick2 = ((iota((kl, levels), 0) & (levels - 1)) == iota((kl, levels), 1)).astype(F32)
    same_k = ((iota((kl, kl), 0) >> ls) == (iota((kl, kl), 1) >> ls)).astype(F32)

    def nt(a, b):
        return lax.dot_general(a, b, NT, precision=HIGHEST, preferred_element_type=F32)

    for i in (0, 1):
        def left(p):
            return jnp.dot(p, lo, precision=HIGHEST, preferred_element_type=F32) if i == 0 else nt(p, lo)

        hi, low = split(nt(left(pick), pick) * near_x)
        mats[i, 0] = hi
        mats[i, 1] = low
        hi, low = split(nt(left(pick2), pick2) * same_k)
        small[i, 0] = hi
        small[i, 1] = low

    yi = iota((1, ny), 1)
    from_south = jnp.where(yi > 0, 0.25, 0.0).astype(F32)
    from_north = jnp.where(yi < ny - 1, 0.25, 0.0).astype(F32)

    def smooth_y(v):
        return 0.5 * v + (from_south * pltpu.roll(v, 1, 1) + from_north * pltpu.roll(v, ny - 1, 1))

    def mix(src, i, edges):
        big = (mats[i, 0], mats[i, 1])
        for k in range(0, members, 2):
            both = jnp.concatenate(
                [src[k * block:(k + 1) * block, :], src[(k + 1) * block:(k + 2) * block, :]], axis=1
            )
            done = dot3(big, both)
            work[k * block:(k + 1) * block, :] = done[:, :ny]
            work[(k + 1) * block:(k + 2) * block, :] = done[:, ny:]
        side = dot3((small[i, 0], small[i, 1]), jnp.concatenate(edges(), axis=1))
        for j, x in ((0, 0), (1, width - 1)):
            at = pl.ds(x, kl, stride=width)
            work[at, :] = work[at, :] + 0.25 * side[:, j * ny:(j + 1) * ny]
        return side

    def send_mem(d, src, dst, ssem, rsem):
        return pltpu.make_async_remote_copy(
            src_ref=src, dst_ref=dst, send_sem=ssem, recv_sem=rsem,
            device_id=(lax.rem(m + d, n_mem), t), device_id_type=MESH,
        )

    def coefficients():
        code = jnp.concatenate([codes_halo[0], codes[...], codes_halo[1]], axis=0)
        speed = jnp.concatenate([wind_halo[0], wind[...], wind_halo[1]], axis=0)
        n = code.shape[0]
        opened = (code != 1).astype(F32)
        absorb = jnp.where(code == 2, absorbing, 1.0).astype(F32)
        yy = iota(code.shape, 1)
        oe = opened * pltpu.roll(opened, n - 1, 0)
        ow = opened * pltpu.roll(opened, 1, 0)
        on = jnp.where(yy < ny - 1, opened * pltpu.roll(opened, ny - 1, 1), 0.0)
        os = jnp.where(yy > 0, opened * pltpu.roll(opened, 1, 1), 0.0)
        k = diffusion_rate
        center = 1.0 - k * (oe + ow + on + os) - speed * oe
        fwd = (center, (k + pltpu.roll(speed, 1, 0)) * ow, k * oe, k * os, k * on)
        adj = (center, k * ow, (k + speed) * oe, k * os, k * on)
        return absorb, fwd, adj

    def stencil(q, coef):
        center, west, east, south, north = coef
        n = q.shape[0]
        return (
            center * q
            + west * pltpu.roll(q, 1, 0)
            + east * pltpu.roll(q, n - 1, 0)
            + south * pltpu.roll(q, 1, 1)
            + north * pltpu.roll(q, ny - 1, 1)
        )

    def observe(field, e):
        state = jnp.stack(field, axis=0)
        tiles = (
            (cell_halo[0], innov_halo[0], sigma_halo[0], 0, HALO, width - HALO),
            (cell[...], innov[...], sigma[...], HALO, width, 0),
            (cell_halo[1], innov_halo[1], sigma_halo[1], HALO + width, HALO, 0),
        )
        pieces = []
        for where, seen, dev, at, count, offset in tiles:
            hot_y = (iota((ny, nobs), 0) == (where & (ny - 1))).astype(BF16)
            hot_x = (iota((count, nobs), 0) == ((where >> log2(ny)) - offset)).astype(F32)
            part_state = state[:, at:at + count, :].reshape(share * count, ny)
            hi, low = split(part_state)
            got = (mm(hi, hot_y) + mm(low, hot_y)).reshape(share, count, nobs)
            sampled = jnp.sum(got * hot_x[None], axis=1)
            scaled = (sampled - seen) / dev
            weight = jnp.clip(scaled, -huber_delta, huber_delta) / dev
            hi, low = split(weight)
            total = None
            for w in (hi, low):
                spread = (w.astype(F32)[:, None, :] * hot_x[None]).reshape(share * count, nobs).astype(BF16)
                put = lax.dot_general(spread, hot_y, NT, preferred_element_type=F32)
                total = put if total is None else total + put
            pieces.append(total.reshape(share, count, ny))
        return jnp.concatenate(pieces, axis=1)


    def evaluate(e, src, edges):
        mix(src, 0, edges)
        for k in range(members):
            at = pl.ds(k * block, block)
            work[at, :] = smooth_y(work[at, :])
        copies = []
        if e == 0:
            loads[2].wait()
        for d in list(range(1, n_mem)) + [0]:
            who = lax.rem(m + d, n_mem)
            r0 = who * share
            l0 = lax.rem(r0, levels)
            total = jnp.zeros((share, width, ny), F32)
            for k in range(members):
                a = work[pl.ds(pl.multiple_of(k * block + l0 * width, width), share * width), :]
                total += ens[k, pl.ds(r0, share)].astype(F32) * a.reshape(share, width, ny)
            part[e, d] = total
            if d:
                copy = send_mem(d, part.at[e, d], rs_buf.at[e, d], rs_send.at[e, d], rs_recv.at[e, d])
                copy.start()
                copies.append(copy)
        if e == 0:
            for k in range(members):
                ensf[pl.ds(k * rows * width, rows * width), :] = (
                    ens[k].astype(F32).reshape(rows * width, ny)
                )
            for i in (0, 1):
                ens_stage[0, i] = ensf[pl.ds(width - 1 - i, members * rows, stride=width), :].astype(BF16)
                ens_stage[1, i] = ensf[pl.ds(i, members * rows, stride=width), :].astype(BF16)
            for side in (0, 1):
                start_side(side, (6,))
            for side in (0, 1):
                recv_side(side, (1, 2, 3, 4, 5))
            for load in loads[3:]:
                load.wait()
        for copy in copies:
            copy.wait_recv()
        total = part[e, 0]
        for d in range(1, n_mem):
            total = total + rs_buf[e, d]
        inc[e, 0] = total[:, width - HALO:, :]
        inc[e, 1] = total[:, :HALO, :]
        halo = [
            to_side(side, inc.at[e, side], inc_halo.at[e, side], h_send.at[e, side], h_recv.at[e, side])
            for side in (0, 1)
        ]
        for side in (0, 1):
            @pl.when(has[1 - side])
            def _():
                halo[side].start()
        absorb, fwd, adj = coefficients()
        for side in (0, 1):
            @pl.when(has[side])
            def _():
                halo[side].wait_recv()
        whole = jnp.concatenate([inc_halo[e, 0], total, inc_halo[e, 1]], axis=1)
        n = HALO + width + HALO
        fields = [whole[r] for r in range(share)]
        for _ in range(STEPS):
            fields = [absorb * stencil(q, fwd) for q in fields]
        gridded = observe(fields, e)
        fields = [gridded[r] for r in range(share)]
        for _ in range(STEPS):
            fields = [stencil(absorb * p, adj) for p in fields]
        for r in range(share):
            ext[pl.ds(r * n, n), :] = fields[r]
            adj_stage[e, r] = fields[r][HALO:HALO + width]
            ag[e, m, r] = fields[r][HALO:HALO + width]
        marks = (HALO - 1, HALO + width) + ((HALO - 2, HALO + width + 1) if e == 0 else ())
        for i, row in enumerate(marks):
            v = ext[pl.ds(row, share, stride=n), :]
            edge_stage[e, i] = v
            agh[e, m, i] = v
        gathers, fringes = [], []
        lines = pl.ds(0, len(marks))
        for d in range(1, n_mem):
            gathers.append(send_mem(d, adj_stage.at[e], ag.at[e, m], ag_send.at[e, d], ag_recv.at[e, d]))
            fringes.append(
                send_mem(
                    d, edge_stage.at[e, lines], agh.at[e, m, lines], e_send.at[e, d], e_recv.at[e, d]
                )
            )
        for copy in gathers + fringes:
            copy.start()
        for copy in gathers:
            copy.wait_recv()
        half = levels * width
        whole = ag[e].reshape(rows * width, ny)
        for k in range(members):
            at = k * rows * width
            nxt[pl.ds(k * block, block), :] = (
                ensf[pl.ds(at, half), :] * whole[:half] + ensf[pl.ds(at + half, half), :] * whole[half:]
            )
        def term_edges():
            for copy in fringes:
                copy.wait_recv()
            if e == 0:
                for side in (0, 1):
                    recv_side(side, (6,))
            terms = []
            for i in range(len(marks)):
                a = agh[e, :, i].reshape(1, rows, ny)
                p = ens_halo[i % 2, i // 2].astype(F32).reshape(members, rows, ny) * a
                terms.append((p[:, :levels] + p[:, levels:]).reshape(kl, ny))
            parts = terms[:2]
            if e == 0:
                row0 = nxt[pl.ds(0, kl, stride=width), :]
                row1 = nxt[pl.ds(width - 1, kl, stride=width), :]
                parts.append(0.5 * terms[0] + 0.25 * (terms[2] + row0))
                parts.append(0.5 * terms[1] + 0.25 * (terms[3] + row1))
            return parts

        side = mix(nxt, 1, term_edges)

        def drain():
            for copy in copies + gathers + fringes:
                copy.wait_send()
            for s in (0, 1):
                @pl.when(has[1 - s])
                def _():
                    halo[s].wait_send()

        return side, drain

    def control_edges():
        for side in (0, 1):
            recv_side(side, (0,))
        return [ctl_halo[0], ctl_halo[1]]

    side, drain0 = evaluate(0, ctl, control_edges)
    outer = []
    for s in (0, 1):
        f = smooth_y(side[:, (2 + s) * ny:(3 + s) * ny])
        c = ctl_halo[s]
        inside = jnp.where(has[s], 1.0, 0.0).astype(F32)
        outer.append((c - step_length * (c + f)) * inside)
    for k in range(members):
        at = pl.ds(k * block, block)
        c = ctl[at, :]
        nxt[at, :] = c - step_length * (c + smooth_y(work[at, :]))
    _, drain1 = evaluate(1, nxt, lambda: outer)
    for k in range(members):
        at = pl.ds(k * block, block)
        out[at, :] = smooth_y(work[at, :])
    drain0()
    drain1()
    for s in (0, 1):
        @pl.when(has[1 - s])
        def _():
            for copy in first_msgs[s]:
                copy.wait_send()


def body(n_mem, n_tile, ensemble, control, level_loc, wind_speed, cell_codes, obs_cell, innovation, obs_sigma):
    members, rows, width, ny = ensemble.shape
    levels = control.shape[1]
    nobs = obs_cell.shape[0]
    share = rows // n_mem
    kl = members * levels
    block = levels * width
    n = width + 2 * HALO
    vmem = pltpu.VMEM
    dma = pltpu.SemaphoreType.DMA
    scratch = [
        vmem((members, rows, width, ny), BF16),
        vmem((members * block, ny), F32),
        vmem((levels, levels), F32),
        vmem((width, ny), F32),
        vmem((width, ny), jnp.int32),
        vmem((1, nobs), jnp.int32),
        vmem((share, nobs), F32),
        vmem((share, nobs), F32),
        dma((8,)),
        vmem((members * rows * width, ny), F32),
        vmem((members * block, ny), F32),
        vmem((members * block, ny), F32),
        vmem((2, 2, block, block), BF16),
        vmem((2, 2, kl, kl), BF16),
        vmem((2, kl, ny), F32),
        vmem((2, kl, ny), F32),
        vmem((2, HALO, ny), jnp.int32),
        vmem((2, HALO, ny), F32),
        vmem((2, 1, nobs), jnp.int32),
        vmem((2, share, nobs), F32),
        vmem((2, share, nobs), F32),
        vmem((2, 2, members * rows, ny), BF16),
        vmem((2, 2, members * rows, ny), BF16),
        vmem((2, n_mem, share, width, ny), F32),
        vmem((2, n_mem, share, width, ny), F32),
        vmem((2, 2, share, HALO, ny), F32),
        vmem((2, 2, share, HALO, ny), F32),
        vmem((share * n, ny), F32),
        vmem((2, share, width, ny), F32),
        vmem((2, n_mem, share, width, ny), F32),
        vmem((2, 4, share, ny), F32),
        vmem((2, n_mem, 4, share, ny), F32),
        dma((2, 7)), dma((2, 7)),
        dma((2, n_mem)), dma((2, n_mem)),
        dma((2, 2)), dma((2, 2)),
        dma((2, n_mem)), dma((2, n_mem)),
        dma((2, n_mem)), dma((2, n_mem)),
    ]
    whole = pl.BlockSpec(memory_space=pltpu.VMEM)
    result = pl.pallas_call(
        functools.partial(kernel, n_mem, n_tile, members, levels, width, ny, nobs),
        out_shape=jax.ShapeDtypeStruct((members * block, ny), F32),
        in_specs=[pl.BlockSpec(memory_space=pltpu.HBM)] * 8,
        out_specs=whole,
        scratch_shapes=scratch,
        compiler_params=pltpu.CompilerParams(
            collective_id=0, has_side_effects=True, vmem_limit_bytes=48 << 20
        ),
    )(*(pltpu.with_memory_space_constraint(x, pltpu.HBM) for x in (
        ensemble,
        control.reshape(members * block, ny),
        level_loc,
        wind_speed,
        cell_codes,
        obs_cell.reshape(1, nobs),
        innovation.reshape(n_mem, share, nobs),
        obs_sigma.reshape(n_mem, share, nobs),
    )))
    return result.reshape(members, levels, width, ny)


def solution(mesh):
    placed = (
        P("mem", None, "tile", None),
        P("mem", None, "tile", None),
        P(),
        P("tile", None),
        P("tile", None),
        P("tile"),
        P(None, "tile"),
        P(None, "tile"),
    )
    return jax.shard_map(
        functools.partial(body, mesh.shape["mem"], mesh.shape["tile"]),
        mesh=mesh, in_specs=placed, out_specs=P("mem", None, "tile", None), check_vma=False,
    )
```

```python
import functools

import jax
import jax.numpy as jnp
from jax import lax
from jax.experimental import pallas as pl
from jax.experimental.pallas import tpu as pltpu
from jax.sharding import PartitionSpec as P

V = 2
STEPS = 2
HALO = 8

diffusion_rate = 0.12
absorbing = 0.7
step_length = 0.5
huber_delta = 1.0

MESH = pl.DeviceIdType.MESH
F32 = jnp.float32
BF16 = jnp.bfloat16
HIGHEST = lax.Precision.HIGHEST
NT = (((1,), (1,)), ((), ()))


def log2(n):
    assert n & (n - 1) == 0
    return n.bit_length() - 1


def iota(shape, dim):
    return lax.broadcasted_iota(jnp.int32, shape, dim)


def split(x):
    hi = x.astype(BF16)
    return hi, (x - hi.astype(F32)).astype(BF16)


def mm(a, b):
    return jnp.dot(a, b, preferred_element_type=F32)


def dot3(a, b):
    ah, al = a
    bh, bl = split(b)
    return mm(ah, bh) + (mm(ah, bl) + mm(al, bh))


def kernel(
    n_mem, n_tile, members, levels, width, ny, nobs,
    ens_hbm, ctl_hbm, loc_hbm, wind_hbm, codes_hbm, cell_hbm, innov_hbm, sigma_hbm,
    out,
    ens, ctl, loc, wind, codes, cell, innov, sigma, in_sem, hot,
    ensf, work, nxt, mats, small,
    ctl_stage, ctl_halo, codes_halo, wind_halo, cell_halo, innov_halo, sigma_halo,
    ens_stage, ens_halo,
    part, rs_buf, inc, inc_halo, ext, adj_stage, ag, edge_stage, agh,
    r0_send, r0_recv, rs_send, rs_recv, h_send, h_recv, ag_send, ag_recv, e_send, e_recv,
):
    m = lax.axis_index("mem")
    t = lax.axis_index("tile")
    has = (t > 0, t < n_tile - 1)
    rows = V * levels
    share = rows // n_mem
    block = levels * width
    kl = members * levels
    xs = log2(width)

    def tell(dev):
        pl.semaphore_signal(pltpu.get_barrier_semaphore(), inc=1, device_id=dev, device_id_type=MESH)

    for d in range(1, n_mem):
        tell((lax.rem(m + d, n_mem), t))

    @pl.when(has[0])
    def _():
        tell((m, t - 1))

    @pl.when(has[1])
    def _():
        tell((m, t + 1))

    loads = [
        pltpu.make_async_copy(src, dst, in_sem.at[i])
        for i, (src, dst) in enumerate((
            (ctl_hbm, ctl), (loc_hbm, loc), (ens_hbm, ens), (wind_hbm, wind), (codes_hbm, codes),
            (cell_hbm, cell), (innov_hbm.at[m], innov), (sigma_hbm.at[m], sigma),
        ))
    ]
    for i in (1, 0, 2, 3, 4, 5, 6, 7):
        loads[i].start()

    loads[1].wait()
    lo = loc[...]
    pick = (iota((block, levels), 0) >> xs == iota((block, levels), 1)).astype(F32)
    xr, xc = iota((block, block), 0) & (width - 1), iota((block, block), 1) & (width - 1)
    near_x = jnp.where(xr == xc, 0.5, jnp.where(jnp.abs(xr - xc) == 1, 0.25, 0.0)).astype(F32)
    ls = log2(levels)
    pick2 = ((iota((kl, levels), 0) & (levels - 1)) == iota((kl, levels), 1)).astype(F32)
    same_k = ((iota((kl, kl), 0) >> ls) == (iota((kl, kl), 1) >> ls)).astype(F32)

    def nt(a, b):
        return lax.dot_general(a, b, NT, precision=HIGHEST, preferred_element_type=F32)

    for i in (0, 1):
        def left(p):
            return jnp.dot(p, lo, precision=HIGHEST, preferred_element_type=F32) if i == 0 else nt(p, lo)

        hi, low = split(nt(left(pick), pick) * near_x)
        mats[i, 0] = hi
        mats[i, 1] = low
        hi, low = split(nt(left(pick2), pick2) * same_k)
        small[i, 0] = hi
        small[i, 1] = low

    loads[0].wait()

    ctl_stage[0] = ctl[pl.ds(width - 1, kl, stride=width), :]
    ctl_stage[1] = ctl[pl.ds(0, kl, stride=width), :]

    peers = n_mem - 1 + jnp.where(t > 0, 1, 0) + jnp.where(t < n_tile - 1, 1, 0)
    pl.semaphore_wait(pltpu.get_barrier_semaphore(), peers)

    def to_side(side, src, dst, ssem, rsem):
        dev = (m, t + 1) if side == 0 else (m, t - 1)
        return pltpu.make_async_remote_copy(
            src_ref=src, dst_ref=dst, send_sem=ssem, recv_sem=rsem, device_id=dev, device_id_type=MESH
        )

    mine = pl.ds(m * share, share)
    near = (pl.ds(width - HALO, HALO), pl.ds(0, HALO))
    first_msgs = []
    for side in (0, 1):
        pairs = [
            (ctl_stage.at[side], ctl_halo.at[side]),
            (codes_hbm.at[near[side]], codes_halo.at[side]),
            (wind_hbm.at[near[side]], wind_halo.at[side]),
            (cell_hbm, cell_halo.at[side]),
            (innov_hbm.at[m], innov_halo.at[side]),
            (sigma_hbm.at[m], sigma_halo.at[side]),
            (ens_stage.at[side], ens_halo.at[side]),
        ]
        first_msgs.append(
            [to_side(side, s, d, r0_send.at[side, i], r0_recv.at[side, i]) for i, (s, d) in enumerate(pairs)]
        )

    def start_side(side, which):
        @pl.when(has[1 - side])
        def _():
            for i in which:
                first_msgs[side][i].start()

    def recv_side(side, which):
        @pl.when(has[side])
        def _():
            for i in which:
                first_msgs[side][i].wait_recv()

    for side in (0, 1):
        start_side(side, (0,))
    for side in (0, 1):
        start_side(side, (1, 2, 3, 4, 5))

        @pl.when(jnp.logical_not(has[side]))
        def _():
            ctl_halo[side] = jnp.zeros_like(ctl_halo[side])
            codes_halo[side] = jnp.ones_like(codes_halo[side])
            wind_halo[side] = jnp.zeros_like(wind_halo[side])
            cell_halo[side] = jnp.full_like(cell_halo[side], -1)
            innov_halo[side] = jnp.zeros_like(innov_halo[side])
            sigma_halo[side] = jnp.ones_like(sigma_halo[side])
            ens_halo[side] = jnp.zeros_like(ens_halo[side])
            for e in (0, 1):
                inc_halo[e, side] = jnp.zeros_like(inc_halo[e, side])

    yi = iota((1, ny), 1)
    from_south = jnp.where(yi > 0, 0.25, 0.0).astype(F32)
    from_north = jnp.where(yi < ny - 1, 0.25, 0.0).astype(F32)

    def smooth_y(v):
        return 0.5 * v + (from_south * pltpu.roll(v, 1, 1) + from_north * pltpu.roll(v, ny - 1, 1))

    def mix(src, i, edges):
        big = (mats[i, 0], mats[i, 1])
        for k in range(0, members, 2):
            both = jnp.concatenate(
                [src[k * block:(k + 1) * block, :], src[(k + 1) * block:(k + 2) * block, :]], axis=1
            )
            done = dot3(big, both)
            work[k * block:(k + 1) * block, :] = done[:, :ny]
            work[(k + 1) * block:(k + 2) * block, :] = done[:, ny:]
        side = dot3((small[i, 0], small[i, 1]), jnp.concatenate(edges(), axis=1))
        for j, x in ((0, 0), (1, width - 1)):
            at = pl.ds(x, kl, stride=width)
            work[at, :] = work[at, :] + 0.25 * side[:, j * ny:(j + 1) * ny]
        return side

    def send_mem(d, src, dst, ssem, rsem):
        return pltpu.make_async_remote_copy(
            src_ref=src, dst_ref=dst, send_sem=ssem, recv_sem=rsem,
            device_id=(lax.rem(m + d, n_mem), t), device_id_type=MESH,
        )

    def coefficients():
        code = jnp.concatenate([codes_halo[0], codes[...], codes_halo[1]], axis=0)
        speed = jnp.concatenate([wind_halo[0], wind[...], wind_halo[1]], axis=0)
        n = code.shape[0]
        opened = (code != 1).astype(F32)
        absorb = jnp.where(code == 2, absorbing, 1.0).astype(F32)
        yy = iota(code.shape, 1)
        oe = opened * pltpu.roll(opened, n - 1, 0)
        ow = opened * pltpu.roll(opened, 1, 0)
        on = jnp.where(yy < ny - 1, opened * pltpu.roll(opened, ny - 1, 1), 0.0)
        os = jnp.where(yy > 0, opened * pltpu.roll(opened, 1, 1), 0.0)
        k = diffusion_rate
        center = 1.0 - k * (oe + ow + on + os) - speed * oe
        fwd = (center, (k + pltpu.roll(speed, 1, 0)) * ow, k * oe, k * os, k * on)
        adj = (center, k * ow, (k + speed) * oe, k * os, k * on)
        return absorb, fwd, adj

    def stencil(q, coef):
        center, west, east, south, north = coef
        n = q.shape[0]
        return (
            center * q
            + west * pltpu.roll(q, 1, 0)
            + east * pltpu.roll(q, n - 1, 0)
            + south * pltpu.roll(q, 1, 1)
            + north * pltpu.roll(q, ny - 1, 1)
        )

    def observe(field, e):
        state = jnp.stack(field, axis=0)
        tiles = (
            (cell_halo[0], innov_halo[0], sigma_halo[0], 0, HALO, width - HALO),
            (cell[...], innov[...], sigma[...], HALO, width, 0),
            (cell_halo[1], innov_halo[1], sigma_halo[1], HALO + width, HALO, 0),
        )
        pieces = []
        for i, (where, seen, dev, at, count, offset) in enumerate(tiles):
            hot_y = hot[i]
            hot_x = (iota((count, nobs), 0) == ((where >> log2(ny)) - offset)).astype(F32)
            part_state = state[:, at:at + count, :].reshape(share * count, ny)
            hi, low = split(part_state)
            got = (mm(hi, hot_y) + mm(low, hot_y)).reshape(share, count, nobs)
            sampled = jnp.sum(got * hot_x[None], axis=1)
            scaled = (sampled - seen) / dev
            weight = jnp.clip(scaled, -huber_delta, huber_delta) / dev
            hi, low = split(weight)
            total = None
            for w in (hi, low):
                spread = (w.astype(F32)[:, None, :] * hot_x[None]).reshape(share * count, nobs).astype(BF16)
                put = lax.dot_general(spread, hot_y, NT, preferred_element_type=F32)
                total = put if total is None else total + put
            pieces.append(total.reshape(share, count, ny))
        return jnp.concatenate(pieces, axis=1)


    def evaluate(e, src, edges):
        mix(src, 0, edges)
        for k in range(members):
            at = pl.ds(k * block, block)
            work[at, :] = smooth_y(work[at, :])
        copies = []
        if e == 0:
            loads[2].wait()
        for d in list(range(1, n_mem)) + [0]:
            who = lax.rem(m + d, n_mem)
            r0 = who * share
            l0 = lax.rem(r0, levels)
            total = jnp.zeros((share, width, ny), F32)
            for k in range(members):
                a = work[pl.ds(pl.multiple_of(k * block + l0 * width, width), share * width), :]
                total += ens[k, pl.ds(r0, share)].astype(F32) * a.reshape(share, width, ny)
            part[e, d] = total
            if d:
                copy = send_mem(d, part.at[e, d], rs_buf.at[e, d], rs_send.at[e, d], rs_recv.at[e, d])
                copy.start()
                copies.append(copy)
        if e == 0:
            for k in range(members):
                ensf[pl.ds(k * rows * width, rows * width), :] = (
                    ens[k].astype(F32).reshape(rows * width, ny)
                )
            for i in (0, 1):
                ens_stage[0, i] = ensf[pl.ds(width - 1 - i, members * rows, stride=width), :].astype(BF16)
                ens_stage[1, i] = ensf[pl.ds(i, members * rows, stride=width), :].astype(BF16)
            for side in (0, 1):
                start_side(side, (6,))
            for side in (0, 1):
                recv_side(side, (1, 2, 3, 4, 5))
            for load in loads[3:]:
                load.wait()
            for i, where in enumerate((cell_halo[0], cell[...], cell_halo[1])):
                hot[i] = (iota((ny, nobs), 0) == (where & (ny - 1))).astype(BF16)
        for copy in copies:
            copy.wait_recv()
        total = part[e, 0]
        for d in range(1, n_mem):
            total = total + rs_buf[e, d]
        inc[e, 0] = total[:, width - HALO:, :]
        inc[e, 1] = total[:, :HALO, :]
        halo = [
            to_side(side, inc.at[e, side], inc_halo.at[e, side], h_send.at[e, side], h_recv.at[e, side])
            for side in (0, 1)
        ]
        for side in (0, 1):
            @pl.when(has[1 - side])
            def _():
                halo[side].start()
        absorb, fwd, adj = coefficients()
        for side in (0, 1):
            @pl.when(has[side])
            def _():
                halo[side].wait_recv()
        whole = jnp.concatenate([inc_halo[e, 0], total, inc_halo[e, 1]], axis=1)
        n = HALO + width + HALO
        fields = [whole[r] for r in range(share)]
        for _ in range(STEPS):
            fields = [absorb * stencil(q, fwd) for q in fields]
        gridded = observe(fields, e)
        fields = [gridded[r] for r in range(share)]
        for _ in range(STEPS):
            fields = [stencil(absorb * p, adj) for p in fields]
        for r in range(share):
            ext[pl.ds(r * n, n), :] = fields[r]
            adj_stage[e, r] = fields[r][HALO:HALO + width]
            ag[e, m, r] = fields[r][HALO:HALO + width]
        gathers = [
            send_mem(d, adj_stage.at[e], ag.at[e, m], ag_send.at[e, d], ag_recv.at[e, d])
            for d in range(1, n_mem)
        ]
        for copy in gathers:
            copy.start()
        marks = (HALO - 1, HALO + width) + ((HALO - 2, HALO + width + 1) if e == 0 else ())
        for i, row in enumerate(marks):
            v = ext[pl.ds(row, share, stride=n), :]
            edge_stage[e, i] = v
            agh[e, m, i] = v
        fringes = []
        lines = pl.ds(0, len(marks))
        for d in range(1, n_mem):
            fringes.append(
                send_mem(
                    d, edge_stage.at[e, lines], agh.at[e, m, lines], e_send.at[e, d], e_recv.at[e, d]
                )
            )
        for copy in fringes:
            copy.start()
        for copy in gathers:
            copy.wait_recv()
        half = levels * width
        whole = ag[e].reshape(rows * width, ny)
        for k in range(members):
            at = k * rows * width
            nxt[pl.ds(k * block, block), :] = (
                ensf[pl.ds(at, half), :] * whole[:half] + ensf[pl.ds(at + half, half), :] * whole[half:]
            )
        def term_edges():
            for copy in fringes:
                copy.wait_recv()
            if e == 0:
                for side in (0, 1):
                    recv_side(side, (6,))
            terms = []
            for i in range(len(marks)):
                a = agh[e, :, i].reshape(1, rows, ny)
                p = ens_halo[i % 2, i // 2].astype(F32).reshape(members, rows, ny) * a
                terms.append((p[:, :levels] + p[:, levels:]).reshape(kl, ny))
            parts = terms[:2]
            if e == 0:
                row0 = nxt[pl.ds(0, kl, stride=width), :]
                row1 = nxt[pl.ds(width - 1, kl, stride=width), :]
                parts.append(0.5 * terms[0] + 0.25 * (terms[2] + row0))
                parts.append(0.5 * terms[1] + 0.25 * (terms[3] + row1))
            return parts

        side = mix(nxt, 1, term_edges)

        def drain():
            for copy in copies + gathers + fringes:
                copy.wait_send()
            for s in (0, 1):
                @pl.when(has[1 - s])
                def _():
                    halo[s].wait_send()

        return side, drain

    def control_edges():
        for side in (0, 1):
            recv_side(side, (0,))
        return [ctl_halo[0], ctl_halo[1]]

    side, drain0 = evaluate(0, ctl, control_edges)
    outer = []
    for s in (0, 1):
        f = smooth_y(side[:, (2 + s) * ny:(3 + s) * ny])
        c = ctl_halo[s]
        inside = jnp.where(has[s], 1.0, 0.0).astype(F32)
        outer.append((c - step_length * (c + f)) * inside)
    for k in range(members):
        at = pl.ds(k * block, block)
        c = ctl[at, :]
        nxt[at, :] = c - step_length * (c + smooth_y(work[at, :]))
    _, drain1 = evaluate(1, nxt, lambda: outer)
    for k in range(members):
        at = pl.ds(k * block, block)
        out[at, :] = smooth_y(work[at, :])
    drain0()
    drain1()
    for s in (0, 1):
        @pl.when(has[1 - s])
        def _():
            for copy in first_msgs[s]:
                copy.wait_send()


def body(n_mem, n_tile, ensemble, control, level_loc, wind_speed, cell_codes, obs_cell, innovation, obs_sigma):
    members, rows, width, ny = ensemble.shape
    levels = control.shape[1]
    nobs = obs_cell.shape[0]
    share = rows // n_mem
    kl = members * levels
    block = levels * width
    n = width + 2 * HALO
    vmem = pltpu.VMEM
    dma = pltpu.SemaphoreType.DMA
    scratch = [
        vmem((members, rows, width, ny), BF16),
        vmem((members * block, ny), F32),
        vmem((levels, levels), F32),
        vmem((width, ny), F32),
        vmem((width, ny), jnp.int32),
        vmem((1, nobs), jnp.int32),
        vmem((share, nobs), F32),
        vmem((share, nobs), F32),
        dma((8,)),
        vmem((3, ny, nobs), BF16),
        vmem((members * rows * width, ny), F32),
        vmem((members * block, ny), F32),
        vmem((members * block, ny), F32),
        vmem((2, 2, block, block), BF16),
        vmem((2, 2, kl, kl), BF16),
        vmem((2, kl, ny), F32),
        vmem((2, kl, ny), F32),
        vmem((2, HALO, ny), jnp.int32),
        vmem((2, HALO, ny), F32),
        vmem((2, 1, nobs), jnp.int32),
        vmem((2, share, nobs), F32),
        vmem((2, share, nobs), F32),
        vmem((2, 2, members * rows, ny), BF16),
        vmem((2, 2, members * rows, ny), BF16),
        vmem((2, n_mem, share, width, ny), F32),
        vmem((2, n_mem, share, width, ny), F32),
        vmem((2, 2, share, HALO, ny), F32),
        vmem((2, 2, share, HALO, ny), F32),
        vmem((share * n, ny), F32),
        vmem((2, share, width, ny), F32),
        vmem((2, n_mem, share, width, ny), F32),
        vmem((2, 4, share, ny), F32),
        vmem((2, n_mem, 4, share, ny), F32),
        dma((2, 7)), dma((2, 7)),
        dma((2, n_mem)), dma((2, n_mem)),
        dma((2, 2)), dma((2, 2)),
        dma((2, n_mem)), dma((2, n_mem)),
        dma((2, n_mem)), dma((2, n_mem)),
    ]
    whole = pl.BlockSpec(memory_space=pltpu.VMEM)
    result = pl.pallas_call(
        functools.partial(kernel, n_mem, n_tile, members, levels, width, ny, nobs),
        out_shape=jax.ShapeDtypeStruct((members * block, ny), F32),
        in_specs=[pl.BlockSpec(memory_space=pltpu.HBM)] * 8,
        out_specs=whole,
        scratch_shapes=scratch,
        compiler_params=pltpu.CompilerParams(
            collective_id=0, has_side_effects=True, vmem_limit_bytes=48 << 20
        ),
    )(*(pltpu.with_memory_space_constraint(x, pltpu.HBM) for x in (
        ensemble,
        control.reshape(members * block, ny),
        level_loc,
        wind_speed,
        cell_codes,
        obs_cell.reshape(1, nobs),
        innovation.reshape(n_mem, share, nobs),
        obs_sigma.reshape(n_mem, share, nobs),
    )))
    return result.reshape(members, levels, width, ny)


def solution(mesh):
    placed = (
        P("mem", None, "tile", None),
        P("mem", None, "tile", None),
        P(),
        P("tile", None),
        P("tile", None),
        P("tile"),
        P(None, "tile"),
        P(None, "tile"),
    )
    return jax.shard_map(
        functools.partial(body, mesh.shape["mem"], mesh.shape["tile"]),
        mesh=mesh, in_specs=placed, out_specs=P("mem", None, "tile", None), check_vma=False,
    )
```

```python
import functools

import jax
import jax.numpy as jnp
from jax import lax
from jax.experimental import pallas as pl
from jax.experimental.pallas import tpu as pltpu
from jax.sharding import PartitionSpec as P

V = 2
STEPS = 2
HALO = 8

diffusion_rate = 0.12
absorbing = 0.7
step_length = 0.5
huber_delta = 1.0

MESH = pl.DeviceIdType.MESH
F32 = jnp.float32
BF16 = jnp.bfloat16
HIGHEST = lax.Precision.HIGHEST
NT = (((1,), (1,)), ((), ()))


def log2(n):
    assert n & (n - 1) == 0
    return n.bit_length() - 1


def iota(shape, dim):
    return lax.broadcasted_iota(jnp.int32, shape, dim)


def split(x):
    hi = x.astype(BF16)
    return hi, (x - hi.astype(F32)).astype(BF16)


def mm(a, b):
    return jnp.dot(a, b, preferred_element_type=F32)


def dot3(a, b):
    ah, al = a
    bh, bl = split(b)
    return mm(ah, bh) + (mm(ah, bl) + mm(al, bh))


def kernel(
    n_mem, n_tile, members, levels, width, ny, nobs,
    ens_hbm, ctl_hbm, loc_hbm, wind_hbm, codes_hbm, cell_hbm, innov_hbm, sigma_hbm,
    out,
    ens, ctl, loc, wind, codes, cell, innov, sigma, in_sem, hot,
    ensf, work, nxt, mats, small,
    ctl_stage, ctl_halo, codes_halo, wind_halo, cell_halo, innov_halo, sigma_halo,
    ens_stage, ens_halo,
    part, rs_buf, inc, inc_halo, ext, adj_stage, ag, edge_stage, agh,
    r0_send, r0_recv, rs_send, rs_recv, h_send, h_recv, ag_send, ag_recv, e_send, e_recv,
):
    m = lax.axis_index("mem")
    t = lax.axis_index("tile")
    has = (t > 0, t < n_tile - 1)
    rows = V * levels
    share = rows // n_mem
    block = levels * width
    kl = members * levels
    xs = log2(width)

    def tell(dev):
        pl.semaphore_signal(pltpu.get_barrier_semaphore(), inc=1, device_id=dev, device_id_type=MESH)

    for d in range(1, n_mem):
        tell((lax.rem(m + d, n_mem), t))

    @pl.when(has[0])
    def _():
        tell((m, t - 1))

    @pl.when(has[1])
    def _():
        tell((m, t + 1))

    loads = [
        pltpu.make_async_copy(src, dst, in_sem.at[i])
        for i, (src, dst) in enumerate((
            (ctl_hbm, ctl), (loc_hbm, loc), (ens_hbm, ens), (wind_hbm, wind), (codes_hbm, codes),
            (cell_hbm, cell), (innov_hbm.at[m], innov), (sigma_hbm.at[m], sigma),
        ))
    ]
    for i in range(len(loads)):
        loads[i].start()

    loads[0].wait()

    ctl_stage[0] = ctl[pl.ds(width - 1, kl, stride=width), :]
    ctl_stage[1] = ctl[pl.ds(0, kl, stride=width), :]

    peers = n_mem - 1 + jnp.where(t > 0, 1, 0) + jnp.where(t < n_tile - 1, 1, 0)
    pl.semaphore_wait(pltpu.get_barrier_semaphore(), peers)

    def to_side(side, src, dst, ssem, rsem):
        dev = (m, t + 1) if side == 0 else (m, t - 1)
        return pltpu.make_async_remote_copy(
            src_ref=src, dst_ref=dst, send_sem=ssem, recv_sem=rsem, device_id=dev, device_id_type=MESH
        )

    mine = pl.ds(m * share, share)
    near = (pl.ds(width - HALO, HALO), pl.ds(0, HALO))
    first_msgs = []
    for side in (0, 1):
        pairs = [
            (ctl_stage.at[side], ctl_halo.at[side]),
            (codes_hbm.at[near[side]], codes_halo.at[side]),
            (wind_hbm.at[near[side]], wind_halo.at[side]),
            (cell_hbm, cell_halo.at[side]),
            (innov_hbm.at[m], innov_halo.at[side]),
            (sigma_hbm.at[m], sigma_halo.at[side]),
            (ens_stage.at[side], ens_halo.at[side]),
        ]
        first_msgs.append(
            [to_side(side, s, d, r0_send.at[side, i], r0_recv.at[side, i]) for i, (s, d) in enumerate(pairs)]
        )

    def start_side(side, which):
        @pl.when(has[1 - side])
        def _():
            for i in which:
                first_msgs[side][i].start()

    def recv_side(side, which):
        @pl.when(has[side])
        def _():
            for i in which:
                first_msgs[side][i].wait_recv()

    for side in (0, 1):
        start_side(side, (0,))
    for side in (0, 1):
        start_side(side, (1, 2, 3, 4, 5))

        @pl.when(jnp.logical_not(has[side]))
        def _():
            ctl_halo[side] = jnp.zeros_like(ctl_halo[side])
            codes_halo[side] = jnp.ones_like(codes_halo[side])
            wind_halo[side] = jnp.zeros_like(wind_halo[side])
            cell_halo[side] = jnp.full_like(cell_halo[side], -1)
            innov_halo[side] = jnp.zeros_like(innov_halo[side])
            sigma_halo[side] = jnp.ones_like(sigma_halo[side])
            ens_halo[side] = jnp.zeros_like(ens_halo[side])
            for e in (0, 1):
                inc_halo[e, side] = jnp.zeros_like(inc_halo[e, side])

    loads[1].wait()
    lo = loc[...]
    pick = (iota((block, levels), 0) >> xs == iota((block, levels), 1)).astype(F32)
    xr, xc = iota((block, block), 0) & (width - 1), iota((block, block), 1) & (width - 1)
    near_x = jnp.where(xr == xc, 0.5, jnp.where(jnp.abs(xr - xc) == 1, 0.25, 0.0)).astype(F32)
    ls = log2(levels)
    pick2 = ((iota((kl, levels), 0) & (levels - 1)) == iota((kl, levels), 1)).astype(F32)
    same_k = ((iota((kl, kl), 0) >> ls) == (iota((kl, kl), 1) >> ls)).astype(F32)

    def nt(a, b):
        return lax.dot_general(a, b, NT, precision=HIGHEST, preferred_element_type=F32)

    for i in (0, 1):
        def left(p):
            return jnp.dot(p, lo, precision=HIGHEST, preferred_element_type=F32) if i == 0 else nt(p, lo)

        hi, low = split(nt(left(pick), pick) * near_x)
        mats[i, 0] = hi
        mats[i, 1] = low
        hi, low = split(nt(left(pick2), pick2) * same_k)
        small[i, 0] = hi
        small[i, 1] = low

    yi = iota((1, ny), 1)
    from_south = jnp.where(yi > 0, 0.25, 0.0).astype(F32)
    from_north = jnp.where(yi < ny - 1, 0.25, 0.0).astype(F32)

    def smooth_y(v):
        return 0.5 * v + (from_south * pltpu.roll(v, 1, 1) + from_north * pltpu.roll(v, ny - 1, 1))

    def mix(src, i, edges):
        big = (mats[i, 0], mats[i, 1])
        for k in range(0, members, 2):
            both = jnp.concatenate(
                [src[k * block:(k + 1) * block, :], src[(k + 1) * block:(k + 2) * block, :]], axis=1
            )
            done = dot3(big, both)
            work[k * block:(k + 1) * block, :] = done[:, :ny]
            work[(k + 1) * block:(k + 2) * block, :] = done[:, ny:]
        side = dot3((small[i, 0], small[i, 1]), jnp.concatenate(edges(), axis=1))
        for j, x in ((0, 0), (1, width - 1)):
            at = pl.ds(x, kl, stride=width)
            work[at, :] = work[at, :] + 0.25 * side[:, j * ny:(j + 1) * ny]
        return side

    def send_mem(d, src, dst, ssem, rsem):
        return pltpu.make_async_remote_copy(
            src_ref=src, dst_ref=dst, send_sem=ssem, recv_sem=rsem,
            device_id=(lax.rem(m + d, n_mem), t), device_id_type=MESH,
        )

    def coefficients():
        code = jnp.concatenate([codes_halo[0], codes[...], codes_halo[1]], axis=0)
        speed = jnp.concatenate([wind_halo[0], wind[...], wind_halo[1]], axis=0)
        n = code.shape[0]
        opened = (code != 1).astype(F32)
        absorb = jnp.where(code == 2, absorbing, 1.0).astype(F32)
        yy = iota(code.shape, 1)
        oe = opened * pltpu.roll(opened, n - 1, 0)
        ow = opened * pltpu.roll(opened, 1, 0)
        on = jnp.where(yy < ny - 1, opened * pltpu.roll(opened, ny - 1, 1), 0.0)
        os = jnp.where(yy > 0, opened * pltpu.roll(opened, 1, 1), 0.0)
        k = diffusion_rate
        center = 1.0 - k * (oe + ow + on + os) - speed * oe
        fwd = (center, (k + pltpu.roll(speed, 1, 0)) * ow, k * oe, k * os, k * on)
        adj = (center, k * ow, (k + speed) * oe, k * os, k * on)
        return absorb, fwd, adj

    def stencil(q, coef):
        center, west, east, south, north = coef
        n = q.shape[0]
        return (
            center * q
            + west * pltpu.roll(q, 1, 0)
            + east * pltpu.roll(q, n - 1, 0)
            + south * pltpu.roll(q, 1, 1)
            + north * pltpu.roll(q, ny - 1, 1)
        )

    def observe(field, e):
        state = jnp.stack(field, axis=0)
        tiles = (
            (cell_halo[0], innov_halo[0], sigma_halo[0], 0, HALO, width - HALO),
            (cell[...], innov[...], sigma[...], HALO, width, 0),
            (cell_halo[1], innov_halo[1], sigma_halo[1], HALO + width, HALO, 0),
        )
        pieces = []
        for i, (where, seen, dev, at, count, offset) in enumerate(tiles):
            hot_y = hot[i]
            hot_x = (iota((count, nobs), 0) == ((where >> log2(ny)) - offset)).astype(F32)
            part_state = state[:, at:at + count, :].reshape(share * count, ny)
            hi, low = split(part_state)
            got = (mm(hi, hot_y) + mm(low, hot_y)).reshape(share, count, nobs)
            sampled = jnp.sum(got * hot_x[None], axis=1)
            scaled = (sampled - seen) / dev
            weight = jnp.clip(scaled, -huber_delta, huber_delta) / dev
            hi, low = split(weight)
            total = None
            for w in (hi, low):
                spread = (w.astype(F32)[:, None, :] * hot_x[None]).reshape(share * count, nobs).astype(BF16)
                put = lax.dot_general(spread, hot_y, NT, preferred_element_type=F32)
                total = put if total is None else total + put
            pieces.append(total.reshape(share, count, ny))
        return jnp.concatenate(pieces, axis=1)


    def evaluate(e, src, edges):
        mix(src, 0, edges)
        for k in range(members):
            at = pl.ds(k * block, block)
            work[at, :] = smooth_y(work[at, :])
        copies = []
        if e == 0:
            loads[2].wait()
        for d in list(range(1, n_mem)) + [0]:
            who = lax.rem(m + d, n_mem)
            r0 = who * share
            l0 = lax.rem(r0, levels)
            total = jnp.zeros((share, width, ny), F32)
            for k in range(members):
                a = work[pl.ds(pl.multiple_of(k * block + l0 * width, width), share * width), :]
                total += ens[k, pl.ds(r0, share)].astype(F32) * a.reshape(share, width, ny)
            part[e, d] = total
            if d:
                copy = send_mem(d, part.at[e, d], rs_buf.at[e, d], rs_send.at[e, d], rs_recv.at[e, d])
                copy.start()
                copies.append(copy)
        if e == 0:
            for k in range(members):
                ensf[pl.ds(k * rows * width, rows * width), :] = (
                    ens[k].astype(F32).reshape(rows * width, ny)
                )
            for i in (0, 1):
                ens_stage[0, i] = ensf[pl.ds(width - 1 - i, members * rows, stride=width), :].astype(BF16)
                ens_stage[1, i] = ensf[pl.ds(i, members * rows, stride=width), :].astype(BF16)
            for side in (0, 1):
                start_side(side, (6,))
            for side in (0, 1):
                recv_side(side, (1, 2, 3, 4, 5))
            for load in loads[3:]:
                load.wait()
            for i, where in enumerate((cell_halo[0], cell[...], cell_halo[1])):
                hot[i] = (iota((ny, nobs), 0) == (where & (ny - 1))).astype(BF16)
        for copy in copies:
            copy.wait_recv()
        total = part[e, 0]
        for d in range(1, n_mem):
            total = total + rs_buf[e, d]
        inc[e, 0] = total[:, width - HALO:, :]
        inc[e, 1] = total[:, :HALO, :]
        halo = [
            to_side(side, inc.at[e, side], inc_halo.at[e, side], h_send.at[e, side], h_recv.at[e, side])
            for side in (0, 1)
        ]
        for side in (0, 1):
            @pl.when(has[1 - side])
            def _():
                halo[side].start()
        absorb, fwd, adj = coefficients()
        for side in (0, 1):
            @pl.when(has[side])
            def _():
                halo[side].wait_recv()
        whole = jnp.concatenate([inc_halo[e, 0], total, inc_halo[e, 1]], axis=1)
        n = HALO + width + HALO
        fields = [whole[r] for r in range(share)]
        for _ in range(STEPS):
            fields = [absorb * stencil(q, fwd) for q in fields]
        gridded = observe(fields, e)
        fields = [gridded[r] for r in range(share)]
        for _ in range(STEPS):
            fields = [stencil(absorb * p, adj) for p in fields]
        for r in range(share):
            ext[pl.ds(r * n, n), :] = fields[r]
            adj_stage[e, r] = fields[r][HALO:HALO + width]
            ag[e, m, r] = fields[r][HALO:HALO + width]
        gathers = [
            send_mem(d, adj_stage.at[e], ag.at[e, m], ag_send.at[e, d], ag_recv.at[e, d])
            for d in range(1, n_mem)
        ]
        for copy in gathers:
            copy.start()
        marks = (HALO - 1, HALO + width) + ((HALO - 2, HALO + width + 1) if e == 0 else ())
        for i, row in enumerate(marks):
            v = ext[pl.ds(row, share, stride=n), :]
            edge_stage[e, i] = v
            agh[e, m, i] = v
        fringes = []
        lines = pl.ds(0, len(marks))
        for d in range(1, n_mem):
            fringes.append(
                send_mem(
                    d, edge_stage.at[e, lines], agh.at[e, m, lines], e_send.at[e, d], e_recv.at[e, d]
                )
            )
        for copy in fringes:
            copy.start()
        for copy in gathers:
            copy.wait_recv()
        half = levels * width
        whole = ag[e].reshape(rows * width, ny)
        for k in range(members):
            at = k * rows * width
            nxt[pl.ds(k * block, block), :] = (
                ensf[pl.ds(at, half), :] * whole[:half] + ensf[pl.ds(at + half, half), :] * whole[half:]
            )
        def term_edges():
            for copy in fringes:
                copy.wait_recv()
            if e == 0:
                for side in (0, 1):
                    recv_side(side, (6,))
            terms = []
            for i in range(len(marks)):
                a = agh[e, :, i].reshape(1, rows, ny)
                p = ens_halo[i % 2, i // 2].astype(F32).reshape(members, rows, ny) * a
                terms.append((p[:, :levels] + p[:, levels:]).reshape(kl, ny))
            parts = terms[:2]
            if e == 0:
                row0 = nxt[pl.ds(0, kl, stride=width), :]
                row1 = nxt[pl.ds(width - 1, kl, stride=width), :]
                parts.append(0.5 * terms[0] + 0.25 * (terms[2] + row0))
                parts.append(0.5 * terms[1] + 0.25 * (terms[3] + row1))
            return parts

        side = mix(nxt, 1, term_edges)

        def drain():
            for copy in copies + gathers + fringes:
                copy.wait_send()
            for s in (0, 1):
                @pl.when(has[1 - s])
                def _():
                    halo[s].wait_send()

        return side, drain

    def control_edges():
        for side in (0, 1):
            recv_side(side, (0,))
        return [ctl_halo[0], ctl_halo[1]]

    side, drain0 = evaluate(0, ctl, control_edges)
    outer = []
    for s in (0, 1):
        f = smooth_y(side[:, (2 + s) * ny:(3 + s) * ny])
        c = ctl_halo[s]
        inside = jnp.where(has[s], 1.0, 0.0).astype(F32)
        outer.append((c - step_length * (c + f)) * inside)
    for k in range(members):
        at = pl.ds(k * block, block)
        c = ctl[at, :]
        nxt[at, :] = c - step_length * (c + smooth_y(work[at, :]))
    _, drain1 = evaluate(1, nxt, lambda: outer)
    for k in range(members):
        at = pl.ds(k * block, block)
        out[at, :] = smooth_y(work[at, :])
    drain0()
    drain1()
    for s in (0, 1):
        @pl.when(has[1 - s])
        def _():
            for copy in first_msgs[s]:
                copy.wait_send()


def body(n_mem, n_tile, ensemble, control, level_loc, wind_speed, cell_codes, obs_cell, innovation, obs_sigma):
    members, rows, width, ny = ensemble.shape
    levels = control.shape[1]
    nobs = obs_cell.shape[0]
    share = rows // n_mem
    kl = members * levels
    block = levels * width
    n = width + 2 * HALO
    vmem = pltpu.VMEM
    dma = pltpu.SemaphoreType.DMA
    scratch = [
        vmem((members, rows, width, ny), BF16),
        vmem((members * block, ny), F32),
        vmem((levels, levels), F32),
        vmem((width, ny), F32),
        vmem((width, ny), jnp.int32),
        vmem((1, nobs), jnp.int32),
        vmem((share, nobs), F32),
        vmem((share, nobs), F32),
        dma((8,)),
        vmem((3, ny, nobs), BF16),
        vmem((members * rows * width, ny), F32),
        vmem((members * block, ny), F32),
        vmem((members * block, ny), F32),
        vmem((2, 2, block, block), BF16),
        vmem((2, 2, kl, kl), BF16),
        vmem((2, kl, ny), F32),
        vmem((2, kl, ny), F32),
        vmem((2, HALO, ny), jnp.int32),
        vmem((2, HALO, ny), F32),
        vmem((2, 1, nobs), jnp.int32),
        vmem((2, share, nobs), F32),
        vmem((2, share, nobs), F32),
        vmem((2, 2, members * rows, ny), BF16),
        vmem((2, 2, members * rows, ny), BF16),
        vmem((2, n_mem, share, width, ny), F32),
        vmem((2, n_mem, share, width, ny), F32),
        vmem((2, 2, share, HALO, ny), F32),
        vmem((2, 2, share, HALO, ny), F32),
        vmem((share * n, ny), F32),
        vmem((2, share, width, ny), F32),
        vmem((2, n_mem, share, width, ny), F32),
        vmem((2, 4, share, ny), F32),
        vmem((2, n_mem, 4, share, ny), F32),
        dma((2, 7)), dma((2, 7)),
        dma((2, n_mem)), dma((2, n_mem)),
        dma((2, 2)), dma((2, 2)),
        dma((2, n_mem)), dma((2, n_mem)),
        dma((2, n_mem)), dma((2, n_mem)),
    ]
    whole = pl.BlockSpec(memory_space=pltpu.VMEM)
    result = pl.pallas_call(
        functools.partial(kernel, n_mem, n_tile, members, levels, width, ny, nobs),
        out_shape=jax.ShapeDtypeStruct((members * block, ny), F32),
        in_specs=[pl.BlockSpec(memory_space=pltpu.HBM)] * 8,
        out_specs=whole,
        scratch_shapes=scratch,
        compiler_params=pltpu.CompilerParams(
            collective_id=0, has_side_effects=True, vmem_limit_bytes=48 << 20
        ),
    )(*(pltpu.with_memory_space_constraint(x, pltpu.HBM) for x in (
        ensemble,
        control.reshape(members * block, ny),
        level_loc,
        wind_speed,
        cell_codes,
        obs_cell.reshape(1, nobs),
        innovation.reshape(n_mem, share, nobs),
        obs_sigma.reshape(n_mem, share, nobs),
    )))
    return result.reshape(members, levels, width, ny)


def solution(mesh):
    placed = (
        P("mem", None, "tile", None),
        P("mem", None, "tile", None),
        P(),
        P("tile", None),
        P("tile", None),
        P("tile"),
        P(None, "tile"),
        P(None, "tile"),
    )
    return jax.shard_map(
        functools.partial(body, mesh.shape["mem"], mesh.shape["tile"]),
        mesh=mesh, in_specs=placed, out_specs=P("mem", None, "tile", None), check_vma=False,
    )
```
